32 devices in a mesh: locus: 2 (over x), row: 4 (over y, core), col: 4 (over z).
Axes of the slice: x: 2, y: 2, z: 4, core: 2. Of those that a mesh axis runs over, the one named last changes fastest.
Arguments:
- input_map: bfloat16 [192, 96, 128], P(('locus', 'row'), 'col'), parts along dimension 0, may hold values from -6 to 6
- conv_weights: bfloat16 [2, 4, 3, 3, 128, 128], replicated, may hold values from -0.25 to 0.25
- conv_bias: float32 [2, 4, 128], replicated, may hold values from -3 to 3
Outputs:
- contact_map: bfloat16 [192, 96, 128], P(('locus', 'row'), 'col'), parts along dimension 0
The draws below stay inside these ranges and needn't reach their ends.
There are 2 independent parts, one for each index of `locus`. The reference program is written for one: setup_inputs(seed, part) draws one part's arguments, and reference() takes and returns one part's arrays. A program takes and returns all parts, laid end to end along the dimension named above; an argument that names none is the same for every part. Nothing has to cross between parts.
All inputs are finite; a program needn't handle non-finite values.
Results may differ from the reference program's by a relative error of at most 0.012.
Values may be sent and summed in bfloat16 or wider, within the bound.
A program may use at most 64 MiB of HBM per device.

```python
import jax
import jax.numpy as jnp
from jax import lax

CH = 128
GROUPS = 2
LAYERS = 4
NB = 96


def steps_of(own_key, shape, shards, smallest, top_value):
    loudness = 1.0
    for position, parts in shards:
        steps = jax.random.uniform(jax.random.fold_in(jax.random.fold_in(own_key, 6), position), (parts,), jnp.float32, smallest / len(shards), top_value / len(shards))
        loudness = loudness * jnp.repeat(jnp.exp(steps), shape[position] // parts).reshape((-1,) + (1,) * (len(shape) - 1 - position))
    return loudness


def scatter_about(own_key, dims, spread, limit, split=(), held_as=jnp.bfloat16):
    entries = spread * jax.random.normal(own_key, dims, jnp.float32)
    if split:
        entries = entries * steps_of(own_key, dims, split, -0.22, 0.18)
    return jnp.clip(entries, -limit, limit).astype(held_as)


def setup_inputs(seed: int = 0, part: int = 0) -> dict:
    seeds = jax.random.split(jax.random.key(seed), 4)
    part_keys = jax.random.split(jax.random.fold_in(seeds[3], part), 4)
    return {
        "input_map": scatter_about(part_keys[0], (NB, NB, CH), 1.0, 6.0, ((0, 4), (1, 4))),
        "conv_weights": scatter_about(seeds[1], (GROUPS, LAYERS, 3, 3, CH, CH), (9 * CH // 2) ** -0.5, 0.25),
        "conv_bias": scatter_about(seeds[2], (GROUPS, LAYERS, CH), 0.5, 3.0, (), jnp.float32),
    }


def apply_layer(hidden, weight, bias_row, dilation):
    summed = lax.conv_general_dilated(
        hidden[None].astype(jnp.float32), weight.astype(jnp.float32), (1, 1),
        ((dilation, dilation), (dilation, dilation)), rhs_dilation=(dilation, dilation),
        dimension_numbers=("NHWC", "HWIO", "NHWC"), precision=lax.Precision.HIGHEST)[0]
    return jax.nn.relu(summed + bias_row).astype(jnp.bfloat16)


def reference(input_map, conv_weights, conv_bias):
    carried = input_map
    for group_idx in range(GROUPS):
        hidden = carried
        for layer_idx in range(LAYERS):
            hidden = apply_layer(hidden, conv_weights[group_idx, layer_idx], conv_bias[group_idx, layer_idx], 2 ** layer_idx)
        carried = (carried.astype(jnp.float32) + hidden.astype(jnp.float32)).astype(jnp.bfloat16)
    flipped = jnp.transpose(carried, (1, 0, 2))
    return (0.5 * (carried.astype(jnp.float32) + flipped.astype(jnp.float32))).astype(jnp.bfloat16)
```

```python
import functools

import jax
import jax.numpy as jnp
from jax import lax
from jax.experimental import pallas as pl
from jax.experimental.pallas import tpu as pltpu
from jax.sharding import PartitionSpec as P

SEGMENTS = ((0, 1, 2, 3),)
PAD = 16
CHUNK_ROWS = 832
MESH = pl.DeviceIdType.MESH


def round_up(value, unit):
    return -(-value // unit) * unit


def neighbours():
    return [(dr, dc) for dr in (-1, 0, 1) for dc in (-1, 0, 1) if (dr, dc) != (0, 0)]


def slot_of(dr, dc):
    return (dr + 1) * 3 + (dc + 1)


def trunk(
    shape, plan, rows_n, cols_n,
    input_ref, weight_ref, bias_ref, out_ref,
    taps, acts, own, edge, side, cap, corner, mir_send, mir_recv,
    weight_sem, input_sem, halo_send, halo_recv, mir_sems, mir_rsems, mir_local,
):
    groups, layers, tile_rows, tile_cols = shape
    ratio = rows_n // cols_n
    row = lax.axis_index("row")
    col = lax.axis_index("col")
    width = acts.shape[3]
    row_start = row * tile_rows
    col_start = col * tile_cols

    copies = []
    for k in range(groups * layers):
        for o in range(2):
            cp = pltpu.make_async_copy(
                weight_ref.at[k // layers, k % layers],
                taps.at[k, pl.ds(o, 3), :, :, pl.ds(o * 128, 128)],
                weight_sem.at[k, o],
            )
            copies.append(cp)
    load = pltpu.make_async_copy(input_ref, own.at[0], input_sem)
    load.start()
    for cp in copies:
        cp.start()

    side[...] = jnp.zeros_like(side)
    cap[...] = jnp.zeros_like(cap)
    corner[...] = jnp.zeros_like(corner)

    def exists(dr, dc):
        ok = jnp.bool_(True)
        if dr:
            ok = jnp.logical_and(ok, (row > 0) if dr < 0 else (row < rows_n - 1))
        if dc:
            ok = jnp.logical_and(ok, (col > 0) if dc < 0 else (col < cols_n - 1))
        return ok

    def device(dr, dc):
        return {"row": row + dr, "col": col + dc}

    partners = []
    for s in range(ratio):
        peer_row = ratio * col + s
        peer_col = row // ratio
        same = jnp.logical_and(peer_row == row, peer_col == col)
        partners.append((peer_row, peer_col, same))

    barrier = pltpu.get_barrier_semaphore()
    for dr, dc in neighbours():
        @pl.when(exists(dr, dc))
        def _():
            pl.semaphore_signal(barrier, inc=1, device_id=device(dr, dc), device_id_type=MESH)
    for peer_row, peer_col, same in partners:
        @pl.when(jnp.logical_not(same))
        def _():
            pl.semaphore_signal(
                barrier, inc=1, device_id={"row": peer_row, "col": peer_col}, device_id_type=MESH
            )

    acts[...] = jnp.zeros_like(acts)
    taps[:, 3, :, :, 0:128] = jnp.zeros((groups * layers, 3, 128, 128), jnp.bfloat16)
    taps[:, 0, :, :, 128:256] = jnp.zeros((groups * layers, 3, 128, 128), jnp.bfloat16)

    load.wait()

    def stage_edges(seg, margin, reach):
        value = own[seg].astype(jnp.float32)
        edge[seg, 0, :, :reach, :] = value[:, :reach, :].astype(jnp.bfloat16)
        edge[seg, 1, :, :reach, :] = value[:, tile_cols - reach :, :].astype(jnp.bfloat16)

    def transfer(seg, margin, reach, dr, dc):
        low = pl.ds(0, margin)
        high = pl.ds(tile_rows - margin, margin)
        rows = low if dr < 0 else high
        if dc == 0:
            src = own.at[seg, rows]
            dst = cap.at[seg, 1 if dr < 0 else 0, pl.ds(0, margin)]
        elif dr == 0:
            src = edge.at[seg, 0 if dc < 0 else 1, :, pl.ds(0, reach)]
            dst = side.at[seg, 1 if dc < 0 else 0, :, pl.ds(0, reach)]
        else:
            src = edge.at[seg, 0 if dc < 0 else 1, rows, pl.ds(0, reach)]
            dst = corner.at[
                seg, 1 if dr < 0 else 0, 1 if dc < 0 else 0, pl.ds(0, margin), pl.ds(0, reach)
            ]
        return pltpu.make_async_remote_copy(
            src_ref=src,
            dst_ref=dst,
            send_sem=halo_send.at[seg, slot_of(dr, dc)],
            recv_sem=halo_recv.at[seg, slot_of(-dr, -dc)],
            device_id=device(dr, dc),
            device_id_type=MESH,
        )

    def arrive(seg, margin, reach, dr, dc):
        transfer(seg, margin, reach, -dr, -dc).wait_recv()

    order = [(0, -1), (0, 1), (-1, 0), (1, 0), (-1, -1), (-1, 1), (1, -1), (1, 1)]

    def send_halo(seg, margin, reach):
        for dr, dc in order:
            @pl.when(exists(dr, dc))
            def _():
                transfer(seg, margin, reach, dr, dc).start()

    def wait_halo(seg, margin, reach):
        for dr, dc in order:
            @pl.when(exists(dr, dc))
            def _():
                arrive(seg, margin, reach, dr, dc)

    def wait_sent(seg, margin, reach):
        for dr, dc in order:
            @pl.when(exists(dr, dc))
            def _():
                transfer(seg, margin, reach, dr, dc).wait_send()

    def spread(buf, at, start, span, value, dilation):
        acts[buf, 1, at, pl.ds(start, span), :] = value.astype(jnp.bfloat16)
        acts[buf, 0, at, pl.ds(start, span), :] = pltpu.roll(value, dilation, 0).astype(jnp.bfloat16)
        acts[buf, 2, at, pl.ds(start, span), :] = pltpu.roll(value, span - dilation, 0).astype(
            jnp.bfloat16
        )

    def assemble(buf, seg, margin, reach, dilation):
        def line(at, left, middle, right):
            parts = []
            if PAD > reach:
                parts.append(jnp.zeros((PAD - reach, 128), jnp.float32))
            parts += [left.astype(jnp.float32), middle.astype(jnp.float32), right.astype(jnp.float32)]
            rest = width - PAD - tile_cols - reach
            if rest:
                parts.append(jnp.zeros((rest, 128), jnp.float32))
            spread(buf, at, 0, width, jnp.concatenate(parts, axis=0), dilation)

        def body_rows(i, carry):
            line(PAD + i, side[seg, 0, i, :reach, :], own[seg, i], side[seg, 1, i, :reach, :])
            return carry

        def cap_rows(i, carry):
            for which, first in ((0, PAD - margin), (1, PAD + tile_rows)):
                line(
                    first + i,
                    corner[seg, which, 0, i, :reach, :],
                    cap[seg, which, i],
                    corner[seg, which, 1, i, :reach, :],
                )
            return carry

        lax.fori_loop(0, tile_rows, body_rows, 0, unroll=2)
        lax.fori_loop(0, margin, cap_rows, 0)

    def layer(k, src, dilation, margin, finish, masked):
        copies[2 * k].wait()
        copies[2 * k + 1].wait()
        start = (PAD - margin) // 16 * 16
        stop = round_up(PAD + tile_cols + margin, 16)
        span = stop - start
        out_rows = tile_rows + 2 * margin
        first = PAD - margin
        blocks = -(-out_rows // (2 * dilation))
        chunk = max(
            n for n in range(1, blocks + 1)
            if blocks % n == 0 and (n == 1 or n * dilation * span <= CHUNK_ROWS)
        )
        bias = bias_ref[pl.ds(k, 1), :]
        if masked:
            col_pos = lax.broadcasted_iota(jnp.int32, (span, 128), 0) + (start - PAD) + col_start
            col_ok = jnp.logical_and(col_pos >= 0, col_pos < tile_cols * cols_n)
            col_scale = jnp.where(col_ok, 1.0, 0.0).astype(jnp.float32)

        def step(c, carry):
            base = first + c * (chunk * 2 * dilation)
            tops = [base + 2 * dilation * b + i for b in range(chunk) for i in range(dilation)]
            lhs = jnp.concatenate(
                [
                    jnp.concatenate(
                        [
                            acts[src, kx, top + (j - 1) * dilation, pl.ds(start, span), :]
                            for j in range(4)
                            for kx in range(3)
                        ],
                        axis=1,
                    )
                    for top in tops
                ],
                axis=0,
            )
            summed = jnp.dot(
                lhs, taps[k].reshape(12 * 128, 256), preferred_element_type=jnp.float32
            )
            for n, top in enumerate(tops):
                for o in range(2):
                    at = top + o * dilation
                    offset = n // dilation * 2 * dilation + n % dilation + o * dilation
                    if blocks == chunk and offset >= out_rows:
                        continue
                    value = summed[n * span : (n + 1) * span, o * 128 : (o + 1) * 128]
                    value = jnp.maximum(value + bias, 0.0)
                    if masked:
                        pos = at - PAD + row_start
                        inside = jnp.logical_and(pos >= 0, pos < tile_rows * rows_n)
                        value = value * (col_scale * jnp.where(inside, 1.0, 0.0))
                    finish(at, start, span, value)
            return carry

        if blocks == chunk:
            step(0, 0)
        else:
            lax.fori_loop(0, blocks // chunk, step, 0)

    seg = 0
    own_slot = 0
    for g in range(groups):
        group_slot = own_slot
        for which, members in enumerate(plan):
            margin = sum(2**l for l in members)
            reach = round_up(margin, 8)
            stage_edges(own_slot, margin, reach)
            if seg == 0:
                count = sum(
                    [jnp.where(exists(dr, dc), 1, 0) for dr, dc in neighbours()]
                    + [jnp.where(same, 0, 1) for _, _, same in partners]
                )
                pl.semaphore_wait(barrier, count)
            send_halo(own_slot, margin, reach)
            wait_halo(own_slot, margin, reach)
            buf = 0
            assemble(buf, own_slot, margin, reach, 2 ** members[0])
            left = margin
            for n, l in enumerate(members):
                left -= 2**l
                last = n == len(members) - 1
                if not last:
                    def finish(at, start, span, value, buf=buf, nxt=2 ** members[n + 1]):
                        spread(1 - buf, at, start, span, value, nxt)
                elif which < len(plan) - 1:
                    def finish(at, start, span, value, dst=own_slot + 1):
                        own[dst, at - PAD] = value[PAD - start : PAD - start + tile_cols].astype(
                            jnp.bfloat16
                        )
                else:
                    def finish(at, start, span, value, src=group_slot, dst=own_slot + 1):
                        hidden = value[PAD - start : PAD - start + tile_cols].astype(jnp.bfloat16)
                        section = own[src, at - PAD].astype(jnp.float32) + hidden.astype(jnp.float32)
                        own[dst, at - PAD] = section.astype(jnp.bfloat16)
                layer(g * layers + l, buf, 2**l, left, finish, masked=not last)
                buf = 1 - buf
            wait_sent(own_slot, margin, reach)
            own_slot += 1
            seg += 1

    final = own_slot
    my_block = row % ratio

    def mirror_copy(s):
        peer_row, peer_col, _ = partners[s]
        return pltpu.make_async_remote_copy(
            src_ref=mir_send.at[s],
            dst_ref=mir_recv.at[my_block],
            send_sem=mir_sems.at[s],
            recv_sem=mir_rsems.at[my_block],
            device_id={"row": peer_row, "col": peer_col},
            device_id_type=MESH,
        )

    value = own[final].astype(jnp.float32)
    for s in range(ratio):
        mir_send[s] = value[:, s * tile_rows : (s + 1) * tile_rows, :].astype(jnp.bfloat16)
        same = partners[s][2]

        @pl.when(jnp.logical_not(same))
        def _():
            mirror_copy(s).start()

        @pl.when(same)
        def _():
            cp = pltpu.make_async_copy(mir_send.at[s], mir_recv.at[my_block], mir_local)
            cp.start()
            cp.wait()
    for s in range(ratio):
        same = partners[s][2]

        @pl.when(jnp.logical_not(same))
        def _():
            pltpu.make_async_remote_copy(
                src_ref=mir_send.at[s],
                dst_ref=mir_recv.at[s],
                send_sem=mir_sems.at[s],
                recv_sem=mir_rsems.at[s],
                device_id={"row": partners[s][0], "col": partners[s][1]},
                device_id_type=MESH,
            ).wait_recv()
            mirror_copy(s).wait_send()
        flipped = jnp.transpose(mir_recv[s].astype(jnp.float32), (1, 0, 2))
        mine = own[final, :, pl.ds(s * tile_rows, tile_rows), :].astype(jnp.float32)
        out_ref[:, pl.ds(s * tile_rows, tile_rows), :] = (0.5 * (mine + flipped)).astype(jnp.bfloat16)


def solution(mesh):
    rows_n = mesh.shape["row"]
    cols_n = mesh.shape["col"]

    def body(input_map, conv_weights, conv_bias):
        tile_rows, tile_cols, channels = input_map.shape
        groups, layers = conv_weights.shape[:2]
        plan = SEGMENTS
        slots = groups * len(plan) + 1
        margin = max(sum(2**l for l in members) for members in plan)
        reach = round_up(margin, 8)
        ratio = rows_n // cols_n
        rows_held = tile_rows + 2 * PAD + 16
        width = round_up(tile_cols + 2 * PAD, 16)
        bf16 = jnp.bfloat16
        kernel = functools.partial(
            trunk, (groups, layers, tile_rows, tile_cols), plan, rows_n, cols_n
        )
        return pl.pallas_call(
            kernel,
            out_shape=jax.ShapeDtypeStruct(input_map.shape, bf16),
            in_specs=[
                pl.BlockSpec(memory_space=pl.ANY),
                pl.BlockSpec(memory_space=pl.ANY),
                pl.BlockSpec(memory_space=pltpu.VMEM),
            ],
            out_specs=pl.BlockSpec(memory_space=pltpu.VMEM),
            scratch_shapes=[
                pltpu.VMEM((groups * layers, 4, 3, channels, 2 * channels), bf16),
                pltpu.VMEM((2, 3, rows_held, width, channels), bf16),
                pltpu.VMEM((slots, tile_rows, tile_cols, channels), bf16),
                pltpu.VMEM((slots, 2, tile_rows, reach, channels), bf16),
                pltpu.VMEM((slots, 2, tile_rows, reach, channels), bf16),
                pltpu.VMEM((slots, 2, margin, tile_cols, channels), bf16),
                pltpu.VMEM((slots, 2, 2, margin, reach, channels), bf16),
                pltpu.VMEM((ratio, tile_rows, tile_rows, channels), bf16),
                pltpu.VMEM((ratio, tile_rows, tile_rows, channels), bf16),
                pltpu.SemaphoreType.DMA((groups * layers, 2)),
                pltpu.SemaphoreType.DMA,
                pltpu.SemaphoreType.DMA((slots, 9)),
                pltpu.SemaphoreType.DMA((slots, 9)),
                pltpu.SemaphoreType.DMA((ratio,)),
                pltpu.SemaphoreType.DMA((ratio,)),
                pltpu.SemaphoreType.DMA,
            ],
            compiler_params=pltpu.CompilerParams(
                collective_id=0, has_side_effects=True, vmem_limit_bytes=60 * 1024 * 1024
            ),
        )(input_map, conv_weights, conv_bias.reshape(groups * layers, channels))

    return jax.shard_map(
        body,
        mesh=mesh,
        in_specs=(P(("locus", "row"), "col", None), P(), P()),
        out_specs=P(("locus", "row"), "col", None),
        check_vma=False,
    )
```

```python
import functools

import jax
import jax.numpy as jnp
from jax import lax
from jax.experimental import pallas as pl
from jax.experimental.pallas import tpu as pltpu
from jax.sharding import PartitionSpec as P

SEGMENTS = ((0, 1, 2, 3),)
PAD = 16
CHUNK_ROWS = 1664
SUB = 13
MESH = pl.DeviceIdType.MESH


def round_up(value, unit):
    return -(-value // unit) * unit


def neighbours():
    return [(dr, dc) for dr in (-1, 0, 1) for dc in (-1, 0, 1) if (dr, dc) != (0, 0)]


def slot_of(dr, dc):
    return (dr + 1) * 3 + (dc + 1)


def trunk(
    shape, plan, rows_n, cols_n,
    input_ref, weight_ref, bias_ref, out_ref,
    taps, acts_a, acts_b, own, edge, side, cap, corner, mir_send, mir_recv,
    weight_sem, input_sem, halo_send, halo_recv, mir_sems, mir_rsems, mir_local,
    detour, detour_send, detour_recv, onward_send, onward_recv,
):
    groups, layers, tile_rows, tile_cols = shape
    ratio = rows_n // cols_n
    row = lax.axis_index("row")
    col = lax.axis_index("col")
    acts = (acts_a, acts_b)
    width = acts_a.shape[2]
    row_start = row * tile_rows
    col_start = col * tile_cols

    copies = []
    for k in range(groups * layers):
        for o in range(2):
            cp = pltpu.make_async_copy(
                weight_ref.at[k // layers, k % layers],
                taps.at[k, pl.ds(o, 3), :, :, pl.ds(o * 128, 128)],
                weight_sem.at[k, o],
            )
            copies.append(cp)
    load = pltpu.make_async_copy(input_ref, own.at[0], input_sem)
    load.start()
    for cp in copies:
        cp.start()

    side[...] = jnp.zeros_like(side)
    cap[...] = jnp.zeros_like(cap)
    corner[...] = jnp.zeros_like(corner)

    def exists(dr, dc):
        ok = jnp.bool_(True)
        if dr:
            ok = jnp.logical_and(ok, (row > 0) if dr < 0 else (row < rows_n - 1))
        if dc:
            ok = jnp.logical_and(ok, (col > 0) if dc < 0 else (col < cols_n - 1))
        return ok

    def device(dr, dc):
        return {"row": row + dr, "col": col + dc}

    partners = []
    for s in range(ratio):
        peer_row = ratio * col + s
        peer_col = row // ratio
        same = jnp.logical_and(peer_row == row, peer_col == col)
        partners.append((peer_row, peer_col, same))

    direct_rows = tile_rows * 14 // 24
    cuts = [direct_rows + (tile_rows - direct_rows) * n // 2 for n in range(2 + 1)]
    pieces = list(zip(cuts[:-1], cuts[1:]))

    def far(r, c, peer_r, peer_c):
        return jnp.logical_and(r // 2 != peer_r // 2, c != peer_c)

    def between(r, c, peer_r, peer_c):
        return peer_r // 2 * 2 + r % 2, c

    flows = []
    for y in range(rows_n // 2):
        for s in range(ratio):
            src_row = 2 * y + row % 2
            to_row, to_col = ratio * col + s, src_row // ratio
            ok = jnp.logical_and(far(src_row, col, to_row, to_col), to_row // 2 == row // 2)
            flows.append((y, s, (src_row, col), (to_row, to_col), src_row % ratio, ok))
    my_slot = row // 2

    def at_device(place):
        return {"row": place[0], "col": place[1]}

    barrier = pltpu.get_barrier_semaphore()
    for _, _, source, _, _, ok in flows:
        @pl.when(ok)
        def _():
            pl.semaphore_signal(barrier, inc=1, device_id=at_device(source), device_id_type=MESH)
    fars = [far(row, col, peer_row, peer_col) for peer_row, peer_col, _ in partners]
    for (peer_row, peer_col, _), ok in zip(partners, fars):
        @pl.when(ok)
        def _():
            pl.semaphore_signal(
                barrier, inc=1, device_id=at_device(between(peer_row, peer_col, row, col)),
                device_id_type=MESH,
            )
    for dr, dc in neighbours():
        @pl.when(exists(dr, dc))
        def _():
            pl.semaphore_signal(barrier, inc=1, device_id=device(dr, dc), device_id_type=MESH)
    for peer_row, peer_col, same in partners:
        @pl.when(jnp.logical_not(same))
        def _():
            pl.semaphore_signal(
                barrier, inc=1, device_id={"row": peer_row, "col": peer_col}, device_id_type=MESH
            )

    for buf in acts:
        spare = (3, buf.shape[1] - PAD - tile_rows, width, 128)
        buf[:, PAD + tile_rows :] = jnp.zeros(spare, jnp.bfloat16)
    taps[:, 3, :, :, 0:128] = jnp.zeros((groups * layers, 3, 128, 128), jnp.bfloat16)
    taps[:, 0, :, :, 128:256] = jnp.zeros((groups * layers, 3, 128, 128), jnp.bfloat16)

    load.wait()

    def stage_edges(seg, margin, reach):
        value = own[seg].astype(jnp.float32)
        edge[seg, 0, :, :reach, :] = value[:, :reach, :].astype(jnp.bfloat16)
        edge[seg, 1, :, :reach, :] = value[:, tile_cols - reach :, :].astype(jnp.bfloat16)

    def transfer(seg, margin, reach, dr, dc):
        low = pl.ds(0, margin)
        high = pl.ds(tile_rows - margin, margin)
        rows = low if dr < 0 else high
        if dc == 0:
            src = own.at[seg, rows]
            dst = cap.at[seg, 1 if dr < 0 else 0, pl.ds(0, margin)]
        elif dr == 0:
            src = edge.at[seg, 0 if dc < 0 else 1, :, pl.ds(0, reach)]
            dst = side.at[seg, 1 if dc < 0 else 0, :, pl.ds(0, reach)]
        else:
            src = edge.at[seg, 0 if dc < 0 else 1, rows, pl.ds(0, reach)]
            dst = corner.at[
                seg, 1 if dr < 0 else 0, 1 if dc < 0 else 0, pl.ds(0, margin), pl.ds(0, reach)
            ]
        return pltpu.make_async_remote_copy(
            src_ref=src,
            dst_ref=dst,
            send_sem=halo_send.at[seg, slot_of(dr, dc)],
            recv_sem=halo_recv.at[seg, slot_of(-dr, -dc)],
            device_id=device(dr, dc),
            device_id_type=MESH,
        )

    def relayed(dr, dc):
        inner = row % 2 == (0 if dr > 0 else 1)
        return jnp.logical_and(exists(dr, dc), inner)

    def straight(dr, dc):
        if dr == 0 or dc == 0:
            return exists(dr, dc)
        inner = row % 2 == (0 if dr > 0 else 1)
        return jnp.logical_and(exists(dr, dc), jnp.logical_not(inner))

    def forward(seg, margin, reach, dr, dc):
        rows = pl.ds(0, margin) if dr < 0 else pl.ds(tile_rows - margin, margin)
        which = 0 if dc < 0 else 1
        return pltpu.make_async_remote_copy(
            src_ref=side.at[seg, which, rows, pl.ds(0, reach)],
            dst_ref=corner.at[seg, 1 if dr < 0 else 0, which, pl.ds(0, margin), pl.ds(0, reach)],
            send_sem=halo_send.at[seg, slot_of(dr, dc)],
            recv_sem=halo_recv.at[seg, slot_of(-dr, dc)],
            device_id=device(dr, 0),
            device_id_type=MESH,
        )

    def arrive(seg, margin, reach, dr, dc):
        transfer(seg, margin, reach, -dr, -dc).wait_recv()

    order = [(0, -1), (0, 1), (-1, 0), (1, 0), (-1, -1), (-1, 1), (1, -1), (1, 1)]

    corners = order[4:]

    def send_halo(seg, margin, reach):
        for dr, dc in order:
            @pl.when(straight(dr, dc))
            def _():
                transfer(seg, margin, reach, dr, dc).start()

    def wait_halo(seg, margin, reach):
        for dr, dc in order[:2]:
            @pl.when(exists(dr, dc))
            def _():
                arrive(seg, margin, reach, dr, dc)
            for fr in (-1, 1):
                @pl.when(relayed(fr, dc))
                def _():
                    forward(seg, margin, reach, fr, dc).start()
        for dr, dc in order[2:]:
            @pl.when(straight(dr, dc))
            def _():
                arrive(seg, margin, reach, dr, dc)
        for dr, dc in corners:
            @pl.when(relayed(dr, dc))
            def _():
                forward(seg, margin, reach, -dr, dc).wait_recv()

    def wait_sent(seg, margin, reach):
        for dr, dc in order:
            @pl.when(straight(dr, dc))
            def _():
                transfer(seg, margin, reach, dr, dc).wait_send()
        for dr, dc in corners:
            @pl.when(relayed(dr, dc))
            def _():
                forward(seg, margin, reach, dr, dc).wait_send()

    def spread(buf, at, span, value, shifts):
        for kx, shift in enumerate(shifts):
            moved = pltpu.roll(value, value.shape[0] - shift, 0) if shift else value
            acts[buf][kx, at, pl.ds(0, span), :] = moved[:span].astype(jnp.bfloat16)

    def assemble(buf, seg, margin, reach, dilation, span):
        first_col = PAD - margin

        def line(at, left, middle, right):
            parts = []
            if PAD > reach:
                parts.append(jnp.zeros((PAD - reach, 128), jnp.float32))
            parts += [left.astype(jnp.float32), middle.astype(jnp.float32), right.astype(jnp.float32)]
            rest = width - PAD - tile_cols - reach
            if rest:
                parts.append(jnp.zeros((rest, 128), jnp.float32))
            shifts = [first_col + kx * dilation for kx in range(3)]
            spread(buf, at, span, jnp.concatenate(parts, axis=0), shifts)

        def body_rows(i, carry):
            line(PAD + i, side[seg, 0, i, :reach, :], own[seg, i], side[seg, 1, i, :reach, :])
            return carry

        def cap_rows(i, carry):
            for which, first in ((0, PAD - margin), (1, PAD + tile_rows)):
                line(
                    first + i,
                    corner[seg, which, 0, i, :reach, :],
                    cap[seg, which, i],
                    corner[seg, which, 1, i, :reach, :],
                )
            return carry

        lax.fori_loop(0, tile_rows, body_rows, 0, unroll=2)
        lax.fori_loop(0, margin, cap_rows, 0)

    def span_of(margin):
        return round_up(tile_cols + 2 * margin, 16)

    def layer(k, src, dilation, margin, finish, masked):
        copies[2 * k].wait()
        copies[2 * k + 1].wait()
        span = span_of(margin)
        out_rows = tile_rows + 2 * margin
        first = PAD - margin
        blocks = -(-out_rows // (2 * dilation))
        chunk = max(
            n for n in range(1, blocks + 1)
            if blocks % n == 0 and (n == 1 or n * dilation * span <= CHUNK_ROWS)
        )
        bias = bias_ref[pl.ds(k, 1), :]
        if masked:
            col_pos = lax.broadcasted_iota(jnp.int32, (span, 128), 0) + col_start - margin
            col_ok = jnp.logical_and(col_pos >= 0, col_pos < tile_cols * cols_n)
            col_scale = jnp.where(col_ok, 1.0, 0.0).astype(jnp.float32)

        def step(c, carry):
            base = first + c * (chunk * 2 * dilation)
            tops = [base + 2 * dilation * b + i for b in range(chunk) for i in range(dilation)]
            parts = [tops[n : n + SUB] for n in range(0, len(tops), SUB)]
            for part, group in enumerate(parts):
                lhs = jnp.concatenate(
                    [
                        jnp.concatenate(
                            [
                                acts[src][kx, top + (j - 1) * dilation, pl.ds(0, span), :]
                                for j in range(4)
                                for kx in range(3)
                            ],
                            axis=1,
                        )
                        for top in group
                    ],
                    axis=0,
                )
                summed = jnp.dot(
                    lhs, taps[k].reshape(12 * 128, 256), preferred_element_type=jnp.float32
                )
                for m, top in enumerate(group):
                    n = part * SUB + m
                    for o in range(2):
                        at = top + o * dilation
                        offset = n // dilation * 2 * dilation + n % dilation + o * dilation
                        if blocks == chunk and offset >= out_rows:
                            continue
                        value = summed[m * span : (m + 1) * span, o * 128 : (o + 1) * 128]
                        value = jnp.maximum(value + bias, 0.0)
                        if masked:
                            pos = at - PAD + row_start
                            inside = jnp.logical_and(pos >= 0, pos < tile_rows * rows_n)
                            value = value * (col_scale * jnp.where(inside, 1.0, 0.0))
                        finish(at, value)
            return carry

        if blocks == chunk:
            step(0, 0)
        else:
            lax.fori_loop(0, blocks // chunk, step, 0)

    seg = 0
    own_slot = 0
    for g in range(groups):
        group_slot = own_slot
        for which, members in enumerate(plan):
            margin = sum(2**l for l in members)
            reach = round_up(margin, 8)
            stage_edges(own_slot, margin, reach)
            if seg == 0:
                count = sum(
                    [jnp.where(exists(dr, dc), 1, 0) for dr, dc in neighbours()]
                    + [jnp.where(same, 0, 1) for _, _, same in partners]
                    + [jnp.where(ok, 1, 0) for ok in fars]
                    + [jnp.where(flow[-1], 1, 0) for flow in flows]
                )
                pl.semaphore_wait(barrier, count)
            send_halo(own_slot, margin, reach)
            wait_halo(own_slot, margin, reach)
            buf = 0
            assemble(
                buf, own_slot, margin, reach, 2 ** members[0], span_of(margin - 2 ** members[0])
            )
            left = margin
            for n, l in enumerate(members):
                left -= 2**l
                last = n == len(members) - 1
                if not last:
                    def finish(at, value, buf=buf, nxt=2 ** members[n + 1], margin=left):
                        spread(1 - buf, at, span_of(margin - nxt), value, [0, nxt, 2 * nxt])
                elif which < len(plan) - 1:
                    def finish(at, value, dst=own_slot + 1):
                        own[dst, at - PAD] = value[:tile_cols].astype(
                            jnp.bfloat16
                        )
                else:
                    def finish(at, value, src=group_slot, dst=own_slot + 1):
                        hidden = value[:tile_cols].astype(jnp.bfloat16)
                        section = own[src, at - PAD].astype(jnp.float32) + hidden.astype(jnp.float32)
                        own[dst, at - PAD] = section.astype(jnp.bfloat16)
                layer(g * layers + l, buf, 2**l, left, finish, masked=not last)
                buf = 1 - buf
            wait_sent(own_slot, margin, reach)
            own_slot += 1
            seg += 1

    final = own_slot
    my_block = row % ratio

    def mirror_copy(s, block, count):
        return pltpu.make_async_remote_copy(
            src_ref=mir_send.at[s, pl.ds(0, count)],
            dst_ref=mir_recv.at[block, pl.ds(0, count)],
            send_sem=mir_sems.at[s],
            recv_sem=mir_rsems.at[block],
            device_id=at_device(partners[s][:2]),
            device_id_type=MESH,
        )

    def to_between(s, n):
        low, high = pieces[n]
        return pltpu.make_async_remote_copy(
            src_ref=mir_send.at[s, pl.ds(low, high - low)],
            dst_ref=detour.at[my_slot, s, pl.ds(low - direct_rows, high - low)],
            send_sem=detour_send.at[s, n],
            recv_sem=detour_recv.at[my_slot, s, n],
            device_id=at_device(between(row, col, *partners[s][:2])),
            device_id_type=MESH,
        )

    def onward(slot, s, target, block, n):
        low, high = pieces[n]
        return pltpu.make_async_remote_copy(
            src_ref=detour.at[slot, s, pl.ds(low - direct_rows, high - low)],
            dst_ref=mir_recv.at[block, pl.ds(low, high - low)],
            send_sem=onward_send.at[slot, s, n],
            recv_sem=onward_recv.at[block, n],
            device_id=at_device(target),
            device_id_type=MESH,
        )

    def arrived_between(slot, s, source, n):
        low, high = pieces[n]
        return pltpu.make_async_remote_copy(
            src_ref=mir_send.at[s, pl.ds(low, high - low)],
            dst_ref=detour.at[slot, s, pl.ds(low - direct_rows, high - low)],
            send_sem=detour_send.at[s, n],
            recv_sem=detour_recv.at[slot, s, n],
            device_id=at_device(source),
            device_id_type=MESH,
        )

    value = own[final].astype(jnp.float32)
    for s in range(ratio):
        mir_send[s] = value[:, s * tile_rows : (s + 1) * tile_rows, :].astype(jnp.bfloat16)
        same = partners[s][2]
        near = jnp.logical_not(jnp.logical_or(same, fars[s]))

        @pl.when(near)
        def _():
            mirror_copy(s, my_block, tile_rows).start()

        @pl.when(fars[s])
        def _():
            for n in range(len(pieces)):
                to_between(s, n).start()
            mirror_copy(s, my_block, direct_rows).start()

        @pl.when(same)
        def _():
            cp = pltpu.make_async_copy(mir_send.at[s], mir_recv.at[my_block], mir_local)
            cp.start()
            cp.wait()
    for n in range(len(pieces)):
        for slot, s, source, target, block, ok in flows:
            @pl.when(ok)
            def _():
                arrived_between(slot, s, source, n).wait_recv()
                onward(slot, s, target, block, n).start()
    for s in range(ratio):
        near = jnp.logical_not(jnp.logical_or(partners[s][2], fars[s]))

        @pl.when(near)
        def _():
            mirror_copy(s, s, tile_rows).wait_recv()
            mirror_copy(s, my_block, tile_rows).wait_send()

        @pl.when(fars[s])
        def _():
            mirror_copy(s, s, direct_rows).wait_recv()
            mirror_copy(s, my_block, direct_rows).wait_send()
            for n in range(len(pieces)):
                onward(0, s, partners[s][:2], s, n).wait_recv()
                to_between(s, n).wait_send()
        flipped = jnp.transpose(mir_recv[s].astype(jnp.float32), (1, 0, 2))
        mine = own[final, :, pl.ds(s * tile_rows, tile_rows), :].astype(jnp.float32)
        out_ref[:, pl.ds(s * tile_rows, tile_rows), :] = (0.5 * (mine + flipped)).astype(jnp.bfloat16)
    for n in range(len(pieces)):
        for slot, s, source, target, block, ok in flows:
            @pl.when(ok)
            def _():
                onward(slot, s, target, block, n).wait_send()


def solution(mesh):
    rows_n = mesh.shape["row"]
    cols_n = mesh.shape["col"]

    def body(input_map, conv_weights, conv_bias):
        tile_rows, tile_cols, channels = input_map.shape
        groups, layers = conv_weights.shape[:2]
        plan = SEGMENTS
        slots = groups * len(plan) + 1
        margin = max(sum(2**l for l in members) for members in plan)
        reach = round_up(margin, 8)
        ratio = rows_n // cols_n
        rows_held = tile_rows + 2 * PAD + 16
        width = round_up(tile_cols + 2 * PAD, 16)
        bf16 = jnp.bfloat16
        kernel = functools.partial(
            trunk, (groups, layers, tile_rows, tile_cols), plan, rows_n, cols_n
        )
        return pl.pallas_call(
            kernel,
            out_shape=jax.ShapeDtypeStruct(input_map.shape, bf16),
            in_specs=[
                pl.BlockSpec(memory_space=pl.ANY),
                pl.BlockSpec(memory_space=pl.ANY),
                pl.BlockSpec(memory_space=pltpu.VMEM),
            ],
            out_specs=pl.BlockSpec(memory_space=pltpu.VMEM),
            scratch_shapes=[
                pltpu.VMEM((groups * layers, 4, 3, channels, 2 * channels), bf16),
                pltpu.VMEM((3, rows_held, width, channels), bf16),
                pltpu.VMEM((3, rows_held, width, channels), bf16),
                pltpu.VMEM((slots, tile_rows, tile_cols, channels), bf16),
                pltpu.VMEM((slots, 2, tile_rows, reach, channels), bf16),
                pltpu.VMEM((slots, 2, tile_rows, reach, channels), bf16),
                pltpu.VMEM((slots, 2, margin, tile_cols, channels), bf16),
                pltpu.VMEM((slots, 2, 2, margin, reach, channels), bf16),
                pltpu.VMEM((ratio, tile_rows, tile_rows, channels), bf16),
                pltpu.VMEM((ratio, tile_rows, tile_rows, channels), bf16),
                pltpu.SemaphoreType.DMA((groups * layers, 2)),
                pltpu.SemaphoreType.DMA,
                pltpu.SemaphoreType.DMA((slots, 9)),
                pltpu.SemaphoreType.DMA((slots, 9)),
                pltpu.SemaphoreType.DMA((ratio,)),
                pltpu.SemaphoreType.DMA((ratio,)),
                pltpu.SemaphoreType.DMA,
                pltpu.VMEM((rows_n // 2, ratio, tile_rows, tile_rows, channels), bf16),
                pltpu.SemaphoreType.DMA((ratio, 2)),
                pltpu.SemaphoreType.DMA((rows_n // 2, ratio, 2)),
                pltpu.SemaphoreType.DMA((rows_n // 2, ratio, 2)),
                pltpu.SemaphoreType.DMA((ratio, 2)),
            ],
            compiler_params=pltpu.CompilerParams(
                collective_id=0, has_side_effects=True, vmem_limit_bytes=60 * 1024 * 1024
            ),
        )(input_map, conv_weights, conv_bias.reshape(groups * layers, channels))

    return jax.shard_map(
        body,
        mesh=mesh,
        in_specs=(P(("locus", "row"), "col", None), P(), P()),
        out_specs=P(("locus", "row"), "col", None),
        check_vma=False,
    )
```

```python
import functools

import jax
import jax.numpy as jnp
from jax import lax
from jax.experimental import pallas as pl
from jax.experimental.pallas import tpu as pltpu
from jax.sharding import PartitionSpec as P

SEGMENTS = ((0, 1, 2, 3),)
PAD = 16
CHUNK_ROWS = 1664
SUB = 13
MESH = pl.DeviceIdType.MESH


def round_up(value, unit):
    return -(-value // unit) * unit


def neighbours():
    return [(dr, dc) for dr in (-1, 0, 1) for dc in (-1, 0, 1) if (dr, dc) != (0, 0)]


def slot_of(dr, dc):
    return (dr + 1) * 3 + (dc + 1)


def trunk(
    shape, plan, rows_n, cols_n,
    input_ref, weight_ref, bias_ref, out_ref,
    taps, acts_a, acts_b, own, edge, side, cap, corner, mir_send, mir_recv,
    weight_sem, input_sem, halo_send, halo_recv, mir_sems, mir_rsems, mir_local,
    detour, detour_send, detour_recv, onward_send, onward_recv,
):
    groups, layers, tile_rows, tile_cols = shape
    ratio = rows_n // cols_n
    row = lax.axis_index("row")
    col = lax.axis_index("col")
    acts = (acts_a, acts_b)
    width = acts_a.shape[2]
    row_start = row * tile_rows
    col_start = col * tile_cols

    copies = []
    for k in range(groups * layers):
        for o in range(2):
            cp = pltpu.make_async_copy(
                weight_ref.at[k // layers, k % layers],
                taps.at[k, pl.ds(o, 3), :, :, pl.ds(o * 128, 128)],
                weight_sem.at[k, o],
            )
            copies.append(cp)
    load = pltpu.make_async_copy(input_ref, own.at[0], input_sem)
    load.start()
    for cp in copies:
        cp.start()

    side[...] = jnp.zeros_like(side)
    cap[...] = jnp.zeros_like(cap)
    corner[...] = jnp.zeros_like(corner)

    def exists(dr, dc):
        ok = jnp.bool_(True)
        if dr:
            ok = jnp.logical_and(ok, (row > 0) if dr < 0 else (row < rows_n - 1))
        if dc:
            ok = jnp.logical_and(ok, (col > 0) if dc < 0 else (col < cols_n - 1))
        return ok

    def device(dr, dc):
        return {"row": row + dr, "col": col + dc}

    partners = []
    for s in range(ratio):
        peer_row = ratio * col + s
        peer_col = row // ratio
        same = jnp.logical_and(peer_row == row, peer_col == col)
        partners.append((peer_row, peer_col, same))

    direct_rows = tile_rows * 16 // 24
    cuts = [direct_rows + (tile_rows - direct_rows) * n // 2 for n in range(2 + 1)]
    pieces = list(zip(cuts[:-1], cuts[1:]))

    def far(r, c, peer_r, peer_c):
        return jnp.logical_and(r // 2 != peer_r // 2, c != peer_c)

    def between(r, c, peer_r, peer_c):
        return peer_r // 2 * 2 + r % 2, c

    flows = []
    for y in range(rows_n // 2):
        for s in range(ratio):
            src_row = 2 * y + row % 2
            to_row, to_col = ratio * col + s, src_row // ratio
            ok = jnp.logical_and(far(src_row, col, to_row, to_col), to_row // 2 == row // 2)
            flows.append((y, s, (src_row, col), (to_row, to_col), src_row % ratio, ok))
    my_slot = row // 2

    def at_device(place):
        return {"row": place[0], "col": place[1]}

    barrier = pltpu.get_barrier_semaphore()
    for _, _, source, _, _, ok in flows:
        @pl.when(ok)
        def _():
            pl.semaphore_signal(barrier, inc=1, device_id=at_device(source), device_id_type=MESH)
    fars = [far(row, col, peer_row, peer_col) for peer_row, peer_col, _ in partners]
    for (peer_row, peer_col, _), ok in zip(partners, fars):
        @pl.when(ok)
        def _():
            pl.semaphore_signal(
                barrier, inc=1, device_id=at_device(between(peer_row, peer_col, row, col)),
                device_id_type=MESH,
            )
    for dr, dc in neighbours():
        @pl.when(exists(dr, dc))
        def _():
            pl.semaphore_signal(barrier, inc=1, device_id=device(dr, dc), device_id_type=MESH)
    for peer_row, peer_col, same in partners:
        @pl.when(jnp.logical_not(same))
        def _():
            pl.semaphore_signal(
                barrier, inc=1, device_id={"row": peer_row, "col": peer_col}, device_id_type=MESH
            )

    for buf in acts:
        spare = (3, buf.shape[1] - PAD - tile_rows, width, 128)
        buf[:, PAD + tile_rows :] = jnp.zeros(spare, jnp.bfloat16)
    taps[:, 3, :, :, 0:128] = jnp.zeros((groups * layers, 3, 128, 128), jnp.bfloat16)
    taps[:, 0, :, :, 128:256] = jnp.zeros((groups * layers, 3, 128, 128), jnp.bfloat16)

    load.wait()

    def stage_edges(seg, margin, reach):
        value = own[seg].astype(jnp.float32)
        edge[seg, 0, :, :reach, :] = value[:, :reach, :].astype(jnp.bfloat16)
        edge[seg, 1, :, :reach, :] = value[:, tile_cols - reach :, :].astype(jnp.bfloat16)

    def transfer(seg, margin, reach, dr, dc):
        low = pl.ds(0, margin)
        high = pl.ds(tile_rows - margin, margin)
        rows = low if dr < 0 else high
        if dc == 0:
            src = own.at[seg, rows]
            dst = cap.at[seg, 1 if dr < 0 else 0, pl.ds(0, margin)]
        elif dr == 0:
            src = edge.at[seg, 0 if dc < 0 else 1, :, pl.ds(0, reach)]
            dst = side.at[seg, 1 if dc < 0 else 0, :, pl.ds(0, reach)]
        else:
            src = edge.at[seg, 0 if dc < 0 else 1, rows, pl.ds(0, reach)]
            dst = corner.at[
                seg, 1 if dr < 0 else 0, 1 if dc < 0 else 0, pl.ds(0, margin), pl.ds(0, reach)
            ]
        return pltpu.make_async_remote_copy(
            src_ref=src,
            dst_ref=dst,
            send_sem=halo_send.at[seg, slot_of(dr, dc)],
            recv_sem=halo_recv.at[seg, slot_of(-dr, -dc)],
            device_id=device(dr, dc),
            device_id_type=MESH,
        )

    def relayed(dr, dc):
        inner = row % 2 == (0 if dr > 0 else 1)
        return jnp.logical_and(exists(dr, dc), inner)

    def straight(dr, dc):
        if dr == 0 or dc == 0:
            return exists(dr, dc)
        inner = row % 2 == (0 if dr > 0 else 1)
        return jnp.logical_and(exists(dr, dc), jnp.logical_not(inner))

    def forward(seg, margin, reach, dr, dc):
        rows = pl.ds(0, margin) if dr < 0 else pl.ds(tile_rows - margin, margin)
        which = 0 if dc < 0 else 1
        return pltpu.make_async_remote_copy(
            src_ref=side.at[seg, which, rows, pl.ds(0, reach)],
            dst_ref=corner.at[seg, 1 if dr < 0 else 0, which, pl.ds(0, margin), pl.ds(0, reach)],
            send_sem=halo_send.at[seg, slot_of(dr, dc)],
            recv_sem=halo_recv.at[seg, slot_of(-dr, dc)],
            device_id=device(dr, 0),
            device_id_type=MESH,
        )

    def arrive(seg, margin, reach, dr, dc):
        transfer(seg, margin, reach, -dr, -dc).wait_recv()

    order = [(0, -1), (0, 1), (-1, 0), (1, 0), (-1, -1), (-1, 1), (1, -1), (1, 1)]

    corners = order[4:]

    def send_halo(seg, margin, reach):
        for dr, dc in order:
            @pl.when(straight(dr, dc))
            def _():
                transfer(seg, margin, reach, dr, dc).start()

    def wait_halo(seg, margin, reach):
        for dr, dc in order[:2]:
            @pl.when(exists(dr, dc))
            def _():
                arrive(seg, margin, reach, dr, dc)
            for fr in (-1, 1):
                @pl.when(relayed(fr, dc))
                def _():
                    forward(seg, margin, reach, fr, dc).start()
        for dr, dc in order[2:]:
            @pl.when(straight(dr, dc))
            def _():
                arrive(seg, margin, reach, dr, dc)
        for dr, dc in corners:
            @pl.when(relayed(dr, dc))
            def _():
                forward(seg, margin, reach, -dr, dc).wait_recv()

    def wait_sent(seg, margin, reach):
        for dr, dc in order:
            @pl.when(straight(dr, dc))
            def _():
                transfer(seg, margin, reach, dr, dc).wait_send()
        for dr, dc in corners:
            @pl.when(relayed(dr, dc))
            def _():
                forward(seg, margin, reach, dr, dc).wait_send()

    def spread(buf, at, span, value, shifts):
        for kx, shift in enumerate(shifts):
            moved = pltpu.roll(value, value.shape[0] - shift, 0) if shift else value
            acts[buf][kx, at, pl.ds(0, span), :] = moved[:span].astype(jnp.bfloat16)

    def assemble(buf, seg, margin, reach, dilation, span):
        first_col = PAD - margin

        def line(at, left, middle, right):
            parts = []
            if PAD > reach:
                parts.append(jnp.zeros((PAD - reach, 128), jnp.float32))
            parts += [left.astype(jnp.float32), middle.astype(jnp.float32), right.astype(jnp.float32)]
            rest = width - PAD - tile_cols - reach
            if rest:
                parts.append(jnp.zeros((rest, 128), jnp.float32))
            shifts = [first_col + kx * dilation for kx in range(3)]
            spread(buf, at, span, jnp.concatenate(parts, axis=0), shifts)

        def body_rows(i, carry):
            line(PAD + i, side[seg, 0, i, :reach, :], own[seg, i], side[seg, 1, i, :reach, :])
            return carry

        def cap_rows(i, carry):
            for which, first in ((0, PAD - margin), (1, PAD + tile_rows)):
                line(
                    first + i,
                    corner[seg, which, 0, i, :reach, :],
                    cap[seg, which, i],
                    corner[seg, which, 1, i, :reach, :],
                )
            return carry

        lax.fori_loop(0, tile_rows, body_rows, 0, unroll=2)
        lax.fori_loop(0, margin, cap_rows, 0)

    def span_of(margin):
        return round_up(tile_cols + 2 * margin, 16)

    def layer(k, src, dilation, margin, finish, masked):
        copies[2 * k].wait()
        copies[2 * k + 1].wait()
        span = span_of(margin)
        out_rows = tile_rows + 2 * margin
        first = PAD - margin
        blocks = -(-out_rows // (2 * dilation))
        chunk = max(
            n for n in range(1, blocks + 1)
            if blocks % n == 0 and (n == 1 or n * dilation * span <= CHUNK_ROWS)
        )
        bias = bias_ref[pl.ds(k, 1), :]
        if masked:
            col_pos = lax.broadcasted_iota(jnp.int32, (span, 128), 0) + col_start - margin
            col_ok = jnp.logical_and(col_pos >= 0, col_pos < tile_cols * cols_n)
            col_scale = jnp.where(col_ok, 1.0, 0.0).astype(jnp.float32)

        def step(c, carry):
            base = first + c * (chunk * 2 * dilation)
            tops = [base + 2 * dilation * b + i for b in range(chunk) for i in range(dilation)]
            parts = [tops[n : n + SUB] for n in range(0, len(tops), SUB)]
            for part, group in enumerate(parts):
                lhs = jnp.concatenate(
                    [
                        jnp.concatenate(
                            [
                                acts[src][kx, top + (j - 1) * dilation, pl.ds(0, span), :]
                                for j in range(4)
                                for kx in range(3)
                            ],
                            axis=1,
                        )
                        for top in group
                    ],
                    axis=0,
                )
                summed = jnp.dot(
                    lhs, taps[k].reshape(12 * 128, 256), preferred_element_type=jnp.float32
                )
                for m, top in enumerate(group):
                    n = part * SUB + m
                    for o in range(2):
                        at = top + o * dilation
                        offset = n // dilation * 2 * dilation + n % dilation + o * dilation
                        if blocks == chunk and offset >= out_rows:
                            continue
                        value = summed[m * span : (m + 1) * span, o * 128 : (o + 1) * 128]
                        value = jnp.maximum(value + bias, 0.0)
                        if masked:
                            pos = at - PAD + row_start
                            inside = jnp.logical_and(pos >= 0, pos < tile_rows * rows_n)
                            value = value * (col_scale * jnp.where(inside, 1.0, 0.0))
                        finish(at, value)
            return carry

        if blocks == chunk:
            step(0, 0)
        else:
            lax.fori_loop(0, blocks // chunk, step, 0)

    seg = 0
    own_slot = 0
    for g in range(groups):
        group_slot = own_slot
        for which, members in enumerate(plan):
            margin = sum(2**l for l in members)
            reach = round_up(margin, 8)
            stage_edges(own_slot, margin, reach)
            if seg == 0:
                count = sum(
                    [jnp.where(exists(dr, dc), 1, 0) for dr, dc in neighbours()]
                    + [jnp.where(same, 0, 1) for _, _, same in partners]
                    + [jnp.where(ok, 1, 0) for ok in fars]
                    + [jnp.where(flow[-1], 1, 0) for flow in flows]
                )
                pl.semaphore_wait(barrier, count)
            send_halo(own_slot, margin, reach)
            wait_halo(own_slot, margin, reach)
            buf = 0
            assemble(
                buf, own_slot, margin, reach, 2 ** members[0], span_of(margin - 2 ** members[0])
            )
            left = margin
            for n, l in enumerate(members):
                left -= 2**l
                last = n == len(members) - 1
                if not last:
                    def finish(at, value, buf=buf, nxt=2 ** members[n + 1], margin=left):
                        spread(1 - buf, at, span_of(margin - nxt), value, [0, nxt, 2 * nxt])
                elif which < len(plan) - 1:
                    def finish(at, value, dst=own_slot + 1):
                        own[dst, at - PAD] = value[:tile_cols].astype(
                            jnp.bfloat16
                        )
                else:
                    def finish(at, value, src=group_slot, dst=own_slot + 1):
                        hidden = value[:tile_cols].astype(jnp.bfloat16)
                        section = own[src, at - PAD].astype(jnp.float32) + hidden.astype(jnp.float32)
                        own[dst, at - PAD] = section.astype(jnp.bfloat16)
                layer(g * layers + l, buf, 2**l, left, finish, masked=not last)
                buf = 1 - buf
            wait_sent(own_slot, margin, reach)
            own_slot += 1
            seg += 1

    final = own_slot
    my_block = row % ratio

    def mirror_copy(s, block, count):
        return pltpu.make_async_remote_copy(
            src_ref=mir_send.at[s, pl.ds(0, count)],
            dst_ref=mir_recv.at[block, pl.ds(0, count)],
            send_sem=mir_sems.at[s],
            recv_sem=mir_rsems.at[block],
            device_id=at_device(partners[s][:2]),
            device_id_type=MESH,
        )

    def to_between(s, n):
        low, high = pieces[n]
        return pltpu.make_async_remote_copy(
            src_ref=mir_send.at[s, pl.ds(low, high - low)],
            dst_ref=detour.at[my_slot, s, pl.ds(low - direct_rows, high - low)],
            send_sem=detour_send.at[s, n],
            recv_sem=detour_recv.at[my_slot, s, n],
            device_id=at_device(between(row, col, *partners[s][:2])),
            device_id_type=MESH,
        )

    def onward(slot, s, target, block, n):
        low, high = pieces[n]
        return pltpu.make_async_remote_copy(
            src_ref=detour.at[slot, s, pl.ds(low - direct_rows, high - low)],
            dst_ref=mir_recv.at[block, pl.ds(low, high - low)],
            send_sem=onward_send.at[slot, s, n],
            recv_sem=onward_recv.at[block, n],
            device_id=at_device(target),
            device_id_type=MESH,
        )

    def arrived_between(slot, s, source, n):
        low, high = pieces[n]
        return pltpu.make_async_remote_copy(
            src_ref=mir_send.at[s, pl.ds(low, high - low)],
            dst_ref=detour.at[slot, s, pl.ds(low - direct_rows, high - low)],
            send_sem=detour_send.at[s, n],
            recv_sem=detour_recv.at[slot, s, n],
            device_id=at_device(source),
            device_id_type=MESH,
        )

    value = own[final].astype(jnp.float32)
    for s in range(ratio):
        mir_send[s] = value[:, s * tile_rows : (s + 1) * tile_rows, :].astype(jnp.bfloat16)
        same = partners[s][2]
        near = jnp.logical_not(jnp.logical_or(same, fars[s]))

        @pl.when(near)
        def _():
            mirror_copy(s, my_block, tile_rows).start()

        @pl.when(fars[s])
        def _():
            for n in range(len(pieces)):
                to_between(s, n).start()
            mirror_copy(s, my_block, direct_rows).start()

        @pl.when(same)
        def _():
            cp = pltpu.make_async_copy(mir_send.at[s], mir_recv.at[my_block], mir_local)
            cp.start()
            cp.wait()
    for n in range(len(pieces)):
        for slot, s, source, target, block, ok in flows:
            @pl.when(ok)
            def _():
                arrived_between(slot, s, source, n).wait_recv()
                onward(slot, s, target, block, n).start()
    for s in range(ratio):
        near = jnp.logical_not(jnp.logical_or(partners[s][2], fars[s]))

        @pl.when(near)
        def _():
            mirror_copy(s, s, tile_rows).wait_recv()
            mirror_copy(s, my_block, tile_rows).wait_send()

        @pl.when(fars[s])
        def _():
            mirror_copy(s, s, direct_rows).wait_recv()
            mirror_copy(s, my_block, direct_rows).wait_send()
            for n in range(len(pieces)):
                onward(0, s, partners[s][:2], s, n).wait_recv()
                to_between(s, n).wait_send()
        flipped = jnp.transpose(mir_recv[s].astype(jnp.float32), (1, 0, 2))
        mine = own[final, :, pl.ds(s * tile_rows, tile_rows), :].astype(jnp.float32)
        out_ref[:, pl.ds(s * tile_rows, tile_rows), :] = (0.5 * (mine + flipped)).astype(jnp.bfloat16)
    for n in range(len(pieces)):
        for slot, s, source, target, block, ok in flows:
            @pl.when(ok)
            def _():
                onward(slot, s, target, block, n).wait_send()


def solution(mesh):
    rows_n = mesh.shape["row"]
    cols_n = mesh.shape["col"]

    def body(input_map, conv_weights, conv_bias):
        tile_rows, tile_cols, channels = input_map.shape
        groups, layers = conv_weights.shape[:2]
        plan = SEGMENTS
        slots = groups * len(plan) + 1
        margin = max(sum(2**l for l in members) for members in plan)
        reach = round_up(margin, 8)
        ratio = rows_n // cols_n
        rows_held = tile_rows + 2 * PAD + 16
        width = round_up(tile_cols + 2 * PAD, 16)
        bf16 = jnp.bfloat16
        kernel = functools.partial(
            trunk, (groups, layers, tile_rows, tile_cols), plan, rows_n, cols_n
        )
        return pl.pallas_call(
            kernel,
            out_shape=jax.ShapeDtypeStruct(input_map.shape, bf16),
            in_specs=[
                pl.BlockSpec(memory_space=pl.ANY),
                pl.BlockSpec(memory_space=pl.ANY),
                pl.BlockSpec(memory_space=pltpu.VMEM),
            ],
            out_specs=pl.BlockSpec(memory_space=pltpu.VMEM),
            scratch_shapes=[
                pltpu.VMEM((groups * layers, 4, 3, channels, 2 * channels), bf16),
                pltpu.VMEM((3, rows_held, width, channels), bf16),
                pltpu.VMEM((3, rows_held, width, channels), bf16),
                pltpu.VMEM((slots, tile_rows, tile_cols, channels), bf16),
                pltpu.VMEM((slots, 2, tile_rows, reach, channels), bf16),
                pltpu.VMEM((slots, 2, tile_rows, reach, channels), bf16),
                pltpu.VMEM((slots, 2, margin, tile_cols, channels), bf16),
                pltpu.VMEM((slots, 2, 2, margin, reach, channels), bf16),
                pltpu.VMEM((ratio, tile_rows, tile_rows, channels), bf16),
                pltpu.VMEM((ratio, tile_rows, tile_rows, channels), bf16),
                pltpu.SemaphoreType.DMA((groups * layers, 2)),
                pltpu.SemaphoreType.DMA,
                pltpu.SemaphoreType.DMA((slots, 9)),
                pltpu.SemaphoreType.DMA((slots, 9)),
                pltpu.SemaphoreType.DMA((ratio,)),
                pltpu.SemaphoreType.DMA((ratio,)),
                pltpu.SemaphoreType.DMA,
                pltpu.VMEM((rows_n // 2, ratio, tile_rows, tile_rows, channels), bf16),
                pltpu.SemaphoreType.DMA((ratio, 2)),
                pltpu.SemaphoreType.DMA((rows_n // 2, ratio, 2)),
                pltpu.SemaphoreType.DMA((rows_n // 2, ratio, 2)),
                pltpu.SemaphoreType.DMA((ratio, 2)),
            ],
            compiler_params=pltpu.CompilerParams(
                collective_id=0, has_side_effects=True, vmem_limit_bytes=60 * 1024 * 1024
            ),
        )(input_map, conv_weights, conv_bias.reshape(groups * layers, channels))

    return jax.shard_map(
        body,
        mesh=mesh,
        in_specs=(P(("locus", "row"), "col", None), P(), P()),
        out_specs=P(("locus", "row"), "col", None),
        check_vma=False,
    )
```
